512 devices in a mesh: terms: 128 (over y, z_hi, x), rows: 4 (over z_lo, core).
Axes of the slice: x: 4, y: 8, z: 8 (z_hi: 4, z_lo: 2; z = z_hi * 2 + z_lo), core: 2. Of those that a mesh axis runs over, the one named last changes fastest.
Arguments:
- psi: float32 [2, 768, 768], P(None, 'rows'), may hold values from -6 to 6
- left_ops: float32 [128, 768, 768], P('terms', 'rows'), may hold values from -0.21875 to 0.21875
- right_ops: float32 [256, 768, 768], P('terms', 'rows'), may hold values from -0.0625 to 0.0625
- term_count: int32 [128], P('terms'), may hold values from 1 to 3, 192 in all
- right_slot: int32 [384], P('terms'), may hold values from 0 to 1
- sector: int32 [384], P('terms'), may hold values from 0 to 1
- sign_bit: int32 [384], P('terms'), may hold values from 0 to 1
Outputs:
- sigma: float32 [2, 768, 768], P(None, 'rows', 'terms')
The draws below stay inside these ranges and needn't reach their ends.
Inputs may be any that keep to these rules, and one draw needn't show every extreme that they name: Owner o's live terms are its first term_count[o] slots of 3; right_slot, sector and sign_bit of the other slots have no effect.
All inputs are finite; a program needn't handle non-finite values. No bound on the sum of `term_count` on one device may be relied on, other than what follows from the above.
Results may differ from the reference program's by a relative error of at most 0.0003.
Values sent between devices are 32-bit elements; how exact they have to be, the bound alone decides.
No kernel may reach another device: no remote copies, remote signals or barrier semaphores. Data moves between devices by JAX's collectives and lax.ppermute only.
A program may use at most 64 MiB of HBM per device.

```python
import math
import jax
import jax.numpy as jnp
import numpy as np
from jax import lax

M = 768
SECTORS = 2
TERM_DEV = 3
RIGHT_DEV = 2
OWNERS = 128
TERMS = 384
RIGHTS = 256
N_TERMS = 128


def set_ends(entries, rng, least, top_value):
    shape = entries.shape
    place = [jax.random.randint(jax.random.fold_in(rng, axis), (), 0, shape[axis]) for axis in range(len(shape))]
    entries = entries.at[tuple(place)].set(least)
    longest = shape.index(max(shape))
    place[longest] = (place[longest] + 1) % shape[longest]
    return entries.at[tuple(place)].set(top_value)


def spiked(entries, own_key, source, target, blocks, factor):
    def block_of(axis_at):
        return (jnp.arange(entries.shape[axis_at]) // (entries.shape[axis_at] // blocks)).reshape((-1,) + (1,) * (entries.ndim - 1 - axis_at))

    near = jax.random.permutation(own_key, blocks)[block_of(target)]
    far = (block_of(target) + blocks // 2) % blocks
    return jnp.where((block_of(source) == near) | (block_of(source) == far), factor * entries, entries)


def block_levels(key, dims, split, low, largest):
    gain = 1.0
    for dim, shards_of in split:
        steps = jax.random.uniform(jax.random.fold_in(jax.random.fold_in(key, 6), dim), (shards_of,), jnp.float32, low / len(split), largest / len(split))
        gain = gain * jnp.repeat(jnp.exp(steps), dims[dim] // shards_of).reshape((-1,) + (1,) * (len(dims) - 1 - dim))
    return gain


def length_profile(count, total, reach, lean):
    loads = [(1 << 20) // math.isqrt(rank ** lean) + 1 for rank in range(2, count + 1)]
    spare, counts = total - reach - (count - 1), [1] * (count - 1)
    while spare > 0:
        free = [i for i in range(count - 1) if counts[i] < reach]
        pool, budget = sum([loads[i] for i in free]), spare
        for i in free:
            extra = min(reach - counts[i], max(1, budget * loads[i] // pool), spare)
            counts[i] = counts[i] + extra
            spare = spare - extra
    return np.array([reach] + counts)


def ragged(key, count, total, bound, skew):
    if count == 2:
        one = jax.random.randint(key, (), max(1, total - bound), min(bound, total - 1) + 1)
        return jnp.stack([one, total - one])
    lengths = jnp.asarray(length_profile(count, total, bound, skew), jnp.int32)
    couples = (count - 1) // 2
    source_of, sink = lengths[1:1 + 2 * couples:2], lengths[2:2 + 2 * couples:2]
    margin = jnp.minimum(source_of - 1, bound - sink)
    moved = jax.random.randint(jax.random.fold_in(key, 1), (couples,), 0, 1 << 20) % (margin + 1)
    lengths = lengths.at[1:1 + 2 * couples:2].set(source_of - moved).at[2:2 + 2 * couples:2].set(sink + moved)
    return lengths[jax.random.permutation(jax.random.fold_in(key, 2), count)]


def noise(rng, dims, width, reach, split=(), held_as=jnp.bfloat16):
    level = block_levels(rng, dims, split, -0.22, 0.18) if split else 1.0
    entries = jax.random.normal(rng, dims, jnp.float32) * width * level
    return jnp.minimum(jnp.maximum(entries, -reach), reach).astype(held_as)


def heavy_noise(stream_key, dims, scale, limit, pieces, heavy, kind=jnp.bfloat16):
    drawn = scale * jax.random.normal(stream_key, dims, jnp.float32)
    if pieces:
        drawn = drawn * block_levels(stream_key, dims, pieces, -0.22, 0.18)
    return jnp.clip(spiked(drawn, jax.random.fold_in(stream_key, 3), *heavy), -limit, limit).astype(kind)


def setup_inputs(seed: int = 0) -> dict:
    key_list = jax.random.split(jax.random.key(seed), 8)
    return {
        "psi": noise(key_list[0], (SECTORS, M, M), 1.0, 6.0, ((1, 4),), jnp.float32),
        "left_ops": noise(key_list[1], (OWNERS, M, M), M ** -0.5, 0.21875, ((0, 128), (1, 4)), jnp.float32),
        "right_ops": heavy_noise(key_list[2], (RIGHTS, M, M), (M * TERM_DEV * N_TERMS // 2) ** -0.5, 0.0625, ((0, 128), (1, 4)), (0, 1, 128, 5.5), jnp.float32),
        "term_count": ragged(key_list[3], OWNERS, N_TERMS * TERM_DEV // 2, TERM_DEV, 2).astype(jnp.int32),
        "right_slot": set_ends(jax.random.randint(key_list[4], (TERMS,), 0, RIGHT_DEV), jax.random.fold_in(key_list[4], 1), 0, RIGHT_DEV - 1).astype(jnp.int32),
        "sector": set_ends(jax.random.randint(key_list[5], (TERMS,), 0, SECTORS), jax.random.fold_in(key_list[5], 1), 0, SECTORS - 1).astype(jnp.int32),
        "sign_bit": set_ends(jax.random.randint(key_list[6], (TERMS,), 0, 2), jax.random.fold_in(key_list[6], 1), 0, 1).astype(jnp.int32),
    }


highest_mode = lax.Precision.HIGHEST


def reference(psi, left_ops, right_ops, term_count, right_slot, sector, sign_bit):
    owner_count = term_count.shape[0]
    slot_count = right_slot.shape[0] // owner_count
    rights_each = right_ops.shape[0] // owner_count
    sector_count = psi.shape[0]
    half_axis = owner_count // 2

    def one_owner(running, owner_id):
        partner = ((owner_id + half_axis) % owner_count).astype(jnp.int32)
        left_block = lax.dynamic_index_in_dim(left_ops, owner_id, 0, keepdims=False)
        right_blocks = lax.dynamic_slice_in_dim(right_ops, (partner * rights_each).astype(jnp.int32), rights_each, 0)
        first_slot = (owner_id * slot_count).astype(jnp.int32)
        slot_ids = lax.dynamic_slice_in_dim(right_slot, first_slot, slot_count, 0)
        sector_ids = lax.dynamic_slice_in_dim(sector, first_slot, slot_count, 0)
        sign_ids = lax.dynamic_slice_in_dim(sign_bit, first_slot, slot_count, 0)
        is_live = jnp.arange(slot_count, dtype=jnp.int32) < term_count[owner_id]
        term_weight = jnp.where(is_live, 2.0 * sign_ids.astype(jnp.float32) - 1.0, 0.0)
        sector_hit = (sector_ids[None, :] == jnp.arange(sector_count, dtype=jnp.int32)[:, None]).astype(jnp.float32) * term_weight[None, :]
        slot_hit = (slot_ids[:, None] == jnp.arange(rights_each, dtype=jnp.int32)[None, :]).astype(jnp.float32)
        mixing = jnp.dot(sector_hit, slot_hit, precision=highest_mode)
        combined = jnp.einsum("sr,rab->sab", mixing, right_blocks, precision=highest_mode)
        inner_rows = jnp.einsum("ab,sbc->sac", left_block, psi, precision=highest_mode)
        return running + jnp.einsum("sac,sdc->sad", inner_rows, combined, precision=highest_mode), None

    start_value = jnp.zeros(psi.shape, jnp.float32)
    summed, _ = lax.scan(one_owner, start_value, jnp.arange(owner_count, dtype=jnp.int32))
    return summed
```

```python
import jax
import jax.numpy as jnp
from jax import lax
from jax.sharding import Mesh
from jax.sharding import PartitionSpec as P

FINE = ("yh", "yl", "zh", "x", "zl", "c")
SIZES = (4, 2, 4, 4, 2, 2)
TERMS = FINE[:4]
ROWS = FINE[4:]


def shifted(block, axis, distance):
    n = lax.axis_size(axis)
    return lax.ppermute(block, axis, [(i, (i + distance) % n) for i in range(n)])


def from_next_pair(block):
    n = lax.axis_size(("zh", "zl"))
    return lax.ppermute(block, ("zh", "zl"), [(z, (z + (1 if z % 2 else -1)) % n) for z in range(n)])


def by_place(blocks, dim):
    shape = blocks.shape
    pairs = blocks.reshape(*shape[:dim], 2, 2, *shape[dim + 1 :])
    pairs = jnp.where(lax.axis_index("zl") == 1, jnp.flip(pairs, dim), pairs)
    pairs = jnp.where(lax.axis_index("c") == 1, jnp.flip(pairs, dim + 1), pairs)
    return pairs.reshape(shape)


def per_device(psi, left_ops, right_ops, term_count, right_slot, sector, sign_bit):
    sectors, rows, m = psi.shape
    rights = right_ops.shape[0]
    left = shifted(left_ops[0], "yh", 2)
    right_z = shifted(right_ops, "zl", 1)
    psi_z = from_next_pair(psi)
    psi_c = shifted(psi, "c", 1)
    right_c = shifted(right_ops, "c", 1)

    is_live = lax.iota(jnp.int32, right_slot.shape[0]) < term_count[0]
    weight = jnp.where(is_live, 2.0 * sign_bit.astype(jnp.float32) - 1.0, 0.0)
    in_sector = sector[None, :] == lax.iota(jnp.int32, sectors)[:, None]
    in_slot = right_slot[None, :] == lax.iota(jnp.int32, rights)[:, None]
    hit = in_sector[:, None, :] & in_slot[None, :, :]
    mixing = shifted(jnp.sum(jnp.where(hit, weight, 0.0), axis=-1), "yh", 2)

    psi_zc = shifted(psi_z, "c", 1)
    right_zc = shifted(right_z, "c", 1)

    left_x = by_place(left.reshape(rows, 4, rows), 1).reshape(rows, m)
    psi_x = jnp.concatenate([psi, psi_c, psi_z, psi_zc], axis=1)
    inner = jnp.einsum("an,snc->sac", left_x, psi_x, precision=lax.Precision.HIGH)
    right_x = jnp.concatenate([right_ops, right_c, right_z, right_zc], axis=1)
    combined = sum(mixing[:, r, None, None] * right_x[r][None] for r in range(rights))
    part = jnp.einsum("sdc,sac->dsa", combined, inner, precision=lax.Precision.HIGH)

    tall = part.reshape(4, 2, 4, 4, -1, sectors * rows).transpose(3, 1, 0, 2, 4, 5)
    tall = tall.reshape(8, -1, sectors * rows)
    got = lax.all_to_all(tall, ("x", "yl"), 0, 0, tiled=True).sum(axis=0)
    small = by_place(got.reshape(4, 4, -1, sectors * rows), 0)
    small = small.reshape(16, -1, sectors * rows)
    own = lax.all_to_all(small, ("yh", "zh"), 0, 0, tiled=True).sum(axis=0)
    return own.reshape(-1, sectors, rows).transpose(1, 2, 0)


def solution(mesh):
    finer = Mesh(mesh.devices.reshape(SIZES), FINE)
    placed = (
        P(None, ROWS, None),
        P(TERMS, ROWS, None),
        P(TERMS, ROWS, None),
        P(TERMS),
        P(TERMS),
        P(TERMS),
        P(TERMS),
    )
    return jax.shard_map(
        per_device, mesh=finer, in_specs=placed, out_specs=P(None, ROWS, TERMS), check_vma=False
    )
```

```python
import jax
import jax.numpy as jnp
from jax import lax
from jax.experimental import pallas as pl
from jax.experimental.pallas import tpu as pltpu
from jax.sharding import Mesh
from jax.sharding import PartitionSpec as P


FINE = ("yh", "yl", "zh", "x", "zl", "c")
SIZES = (4, 2, 4, 4, 2, 2)
TERMS = FINE[:4]
ROWS = FINE[4:]
VMEM = pl.BlockSpec(memory_space=pltpu.VMEM)
SMEM = pl.BlockSpec(memory_space=pltpu.SMEM)
MIB = 1 << 20


def shifted(block, axis, distance):
    n = lax.axis_size(axis)
    return lax.ppermute(block, axis, [(i, (i + distance) % n) for i in range(n)])


def from_next_pair(block):
    n = lax.axis_size(("zh", "zl"))
    return lax.ppermute(
        block, ("zh", "zl"), [(z, (z + (1 if z % 2 else -1)) % n) for z in range(n)]
    )


def halves(value):
    high = value.astype(jnp.bfloat16)
    return high, (value - high.astype(jnp.float32)).astype(jnp.bfloat16)


def product(a, b, dims):
    return lax.dot_general(a, b, (dims, ((), ())), preferred_element_type=jnp.float32)


def three_pass(a, b, dims):
    return product(a[0], b[0], dims) + (product(a[0], b[1], dims) + product(a[1], b[0], dims))


def mixed(mix, block, s):
    return mix[s, 0] * block[0] + mix[s, 1] * block[1]


ROW = ((1,), (0,))
TURNED = ((1,), (1,))


def split_kernel(place, psi, psi_c, psi_h, psi_l):
    sectors, rows, _ = psi.shape
    for i, p in enumerate((psi, psi_c)):
        at = pl.ds(pl.multiple_of((place[1] ^ i) * rows, rows), rows)
        for s in range(sectors):
            psi_h[s, at, :], psi_l[s, at, :] = halves(p[s])


def mix_kernel(mix, right, right_c, comb_h, comb_l):
    for i, r in enumerate((right, right_c)):
        for s in range(comb_h.shape[1]):
            comb_h[i, s], comb_l[i, s] = halves(mixed(mix, r, s))


def near_kernel(place, left, psi_h, psi_l, near):
    half = psi_h.shape[1]
    mine = halves(left[:, pl.ds(pl.multiple_of(place[0] * half, 128), half)])
    for s in range(psi_h.shape[0]):
        near[s] = three_pass(mine, (psi_h[s], psi_l[s]), ROW)


def next_kernel(psi_z, next_h, next_l):
    for s in range(psi_z.shape[0]):
        next_h[s], next_l[s] = halves(psi_z[s])


def far_kernel(place, left, near, next_h, next_l, psi_zc, inner_h, inner_l):
    sectors, rows, half = psi_zc.shape[0], psi_zc.shape[1], left.shape[1] // 2
    other = left[:, pl.ds(pl.multiple_of((1 - place[0]) * half, 128), half)]
    swapped = jnp.concatenate([other[:, rows:], other[:, :rows]], axis=1)
    other = halves(jnp.where(place[1] == 1, swapped, other))
    for s in range(sectors):
        zc_h, zc_l = halves(psi_zc[s])
        far_h = jnp.concatenate([next_h[s], zc_h], axis=0)
        far_l = jnp.concatenate([next_l[s], zc_l], axis=0)
        inner = near[s] + three_pass(other, (far_h, far_l), ROW)
        inner_h[s], inner_l[s] = halves(inner)


def term_kernel(place, mix, inner_h, inner_l, comb_h, comb_l, right_z, right_zc, out, part, held, sem):
    sectors, _, _ = inner_h.shape
    mine = place[0] * 2 + place[1]
    fetch = pltpu.make_async_copy(right_z, held, sem)
    fetch.start()
    for i in range(4):
        if i == 2:
            fetch.wait()
        both = []
        for s in range(sectors):
            if i < 2:
                comb = comb_h[i, s], comb_l[i, s]
            else:
                comb = halves(mixed(mix, held if i == 2 else right_zc, s))
            both.append(three_pass(comb, (inner_h[s], inner_l[s]), TURNED))
        part[...] = jnp.concatenate(both, axis=1)
        for yl in range(2):
            for zh in range(4):
                for x in range(4):
                    at = yl * 96 + zh * 24 + x * 6
                    out[x * 2 + yl, mine ^ i, zh * 6 : zh * 6 + 6, :] = part[at : at + 6, :]


def call(kernel, shapes, specs, flops, scratch=()):
    step = pl.pallas_call(
        kernel,
        out_shape=shapes,
        in_specs=specs,
        out_specs=jax.tree.map(lambda _: VMEM, shapes),
        scratch_shapes=scratch,
        compiler_params=pltpu.CompilerParams(vmem_limit_bytes=24 * MIB),
        cost_estimate=pl.CostEstimate(flops=flops, bytes_accessed=8 * MIB, transcendentals=0),
    )
    return step


def per_device(psi, left_ops, right_ops, term_count, right_slot, sector, sign_bit):
    sectors, rows, m = psi.shape
    rights = right_ops.shape[0]
    f32, bf16 = jnp.float32, jnp.bfloat16
    shape = jax.ShapeDtypeStruct
    left = shifted(left_ops[0], "yh", 2)
    right_z = shifted(right_ops, "zl", 1)
    psi_z = from_next_pair(psi)
    psi_c = shifted(psi, "c", 1)
    right_c = shifted(right_ops, "c", 1)

    is_live = lax.iota(jnp.int32, right_slot.shape[0]) < term_count[0]
    weight = jnp.where(is_live, 2.0 * sign_bit.astype(f32) - 1.0, 0.0)
    in_sector = sector[None, :] == lax.iota(jnp.int32, sectors)[:, None]
    in_slot = right_slot[None, :] == lax.iota(jnp.int32, rights)[:, None]
    hit = in_sector[:, None, :] & in_slot[None, :, :]
    mixing = shifted(jnp.sum(jnp.where(hit, weight, 0.0), axis=-1), "yh", 2)

    psi_zc = shifted(psi_z, "c", 1)
    right_zc = shifted(right_z, "c", 1)

    place = jnp.stack([lax.axis_index("zl"), lax.axis_index("c")]).astype(jnp.int32)
    product_flops = 2 * sectors * rows * m * m
    prepared = shape((sectors, 2 * rows, m), bf16)
    combined = shape((2, sectors, rows, m), bf16)
    psi_h, psi_l = call(split_kernel, (prepared, prepared), [SMEM] + [VMEM] * 2, MIB)(
        place, psi, psi_c
    )
    comb_h, comb_l = call(mix_kernel, (combined, combined), [SMEM] + [VMEM] * 2, MIB)(
        mixing, right_ops, right_c
    )
    near = call(near_kernel, shape((sectors, rows, m), f32), [SMEM] + [VMEM] * 3, 3 * product_flops // 2)(
        place, left, psi_h, psi_l
    )
    inner = shape((sectors, rows, m), bf16)
    next_h, next_l = call(next_kernel, (inner, inner), [VMEM], MIB)(psi_z)
    inner_h, inner_l = call(
        far_kernel,
        (inner, inner),
        [SMEM] + [VMEM] * 5,
        3 * product_flops // 2,
    )(place, left, near, next_h, next_l, psi_zc)
    tall = call(
        term_kernel,
        shape((8, 4, 24, sectors * rows), f32),
        [SMEM, SMEM] + [VMEM] * 4 + [pl.BlockSpec(memory_space=pl.ANY), VMEM],
        3 * product_flops,
        [
            pltpu.VMEM((rows, sectors * rows), f32),
            pltpu.VMEM((rights, rows, m), f32),
            pltpu.SemaphoreType.DMA,
        ],
    )(place, mixing, inner_h, inner_l, comb_h, comb_l, right_z, right_zc)

    got = lax.all_to_all(tall.reshape(8, -1, sectors * rows), ("x", "yl"), 0, 0, tiled=True)
    small = got.sum(axis=0).reshape(16, -1, sectors * rows)
    own = lax.all_to_all(small, ("yh", "zh"), 0, 0, tiled=True).sum(axis=0)
    return own.reshape(-1, sectors, rows).transpose(1, 2, 0)


def solution(mesh):
    finer = Mesh(mesh.devices.reshape(SIZES), FINE)
    placed = (
        P(None, ROWS, None),
        P(TERMS, ROWS, None),
        P(TERMS, ROWS, None),
        P(TERMS),
        P(TERMS),
        P(TERMS),
        P(TERMS),
    )
    return jax.shard_map(
        per_device, mesh=finer, in_specs=placed, out_specs=P(None, ROWS, TERMS), check_vma=False
    )
```

```python
import jax
import jax.numpy as jnp
from jax import lax
from jax.experimental import pallas as pl
from jax.experimental.pallas import tpu as pltpu
from jax.sharding import Mesh
from jax.sharding import PartitionSpec as P


FINE = ("yh", "yl", "zh", "x", "zl", "c")
SIZES = (4, 2, 4, 4, 2, 2)
TERMS = FINE[:4]
ROWS = FINE[4:]
VMEM = pl.BlockSpec(memory_space=pltpu.VMEM)
SMEM = pl.BlockSpec(memory_space=pltpu.SMEM)
MIB = 1 << 20
GROUPS = ((3, 0), (1, 2))


def shifted(block, axis, distance):
    n = lax.axis_size(axis)
    return lax.ppermute(block, axis, [(i, (i + distance) % n) for i in range(n)])


def from_next_pair(block):
    n = lax.axis_size(("zh", "zl"))
    return lax.ppermute(
        block, ("zh", "zl"), [(z, (z + (1 if z % 2 else -1)) % n) for z in range(n)]
    )


def halves(value):
    high = value.astype(jnp.bfloat16)
    return high, (value - high.astype(jnp.float32)).astype(jnp.bfloat16)


def product(a, b, dims):
    return lax.dot_general(a, b, (dims, ((), ())), preferred_element_type=jnp.float32)


def three_pass(a, b, dims):
    return product(a[0], b[0], dims) + (product(a[0], b[1], dims) + product(a[1], b[0], dims))


def mixed(mix, block, s):
    return mix[s, 0] * block[0] + mix[s, 1] * block[1]


ROW = ((1,), (0,))
TURNED = ((1,), (1,))


def split_kernel(place, psi, psi_c, psi_h, psi_l):
    sectors, rows, _ = psi.shape
    for i, p in enumerate((psi, psi_c)):
        at = pl.ds(pl.multiple_of((place[1] ^ i) * rows, rows), rows)
        for s in range(sectors):
            psi_h[s, at, :], psi_l[s, at, :] = halves(p[s])


def near_kernel(place, left, psi_h, psi_l, near):
    half = psi_h.shape[1]
    mine = halves(left[:, pl.ds(pl.multiple_of(place[0] * half, 128), half)])
    for s in range(psi_h.shape[0]):
        near[s] = three_pass(mine, (psi_h[s], psi_l[s]), ROW)


def next_kernel(psi_z, next_h, next_l):
    for s in range(psi_z.shape[0]):
        next_h[s], next_l[s] = halves(psi_z[s])


def far_kernel(place, left, near, next_h, next_l, psi_zc, inner_h, inner_l):
    sectors, rows, half = psi_zc.shape[0], psi_zc.shape[1], left.shape[1] // 2
    other = left[:, pl.ds(pl.multiple_of((1 - place[0]) * half, 128), half)]
    swapped = jnp.concatenate([other[:, rows:], other[:, :rows]], axis=1)
    other = halves(jnp.where(place[1] == 1, swapped, other))
    for s in range(sectors):
        zc_h, zc_l = halves(psi_zc[s])
        far_h = jnp.concatenate([next_h[s], zc_h], axis=0)
        far_l = jnp.concatenate([next_l[s], zc_l], axis=0)
        inner = near[s] + three_pass(other, (far_h, far_l), ROW)
        inner_h[s], inner_l[s] = halves(inner)


def term_kernel(place, mix, inner_h, inner_l, right, right_c, right_z, right_zc, out, part, held, sems):
    sectors, rows, _ = inner_h.shape
    mine = place[0] * 2 + place[1]
    fetches = [
        pltpu.make_async_copy(block, held.at[i], sems.at[i])
        for i, block in enumerate((right, right_c, right_z))
    ]
    for fetch in fetches:
        fetch.start()
    for group in GROUPS:
        blocks = []
        for i in group:
            if i < 3:
                fetches[i].wait()
            blocks.append(right_zc if i == 3 else held.at[i])
        both = []
        for s in range(sectors):
            parts = [halves(mixed(mix, block, s)) for block in blocks]
            comb = [jnp.concatenate(p, axis=0) for p in zip(*parts)]
            both.append(three_pass(comb, (inner_h[s], inner_l[s]), TURNED))
        for n, i in enumerate(group):
            rows_at = slice(n * rows, (n + 1) * rows)
            part[i] = jnp.concatenate([b[rows_at] for b in both], axis=1)
            for yl in range(2):
                for zh in range(4):
                    for x in range(4):
                        at = yl * 96 + zh * 24 + x * 6
                        out[x * 2 + yl, mine ^ i, zh * 6 : zh * 6 + 6, :] = part[i, at : at + 6, :]


def call(kernel, shapes, specs, flops, scratch=()):
    step = pl.pallas_call(
        kernel,
        out_shape=shapes,
        in_specs=specs,
        out_specs=jax.tree.map(lambda _: VMEM, shapes),
        scratch_shapes=scratch,
        compiler_params=pltpu.CompilerParams(vmem_limit_bytes=24 * MIB),
        cost_estimate=pl.CostEstimate(flops=flops, bytes_accessed=8 * MIB, transcendentals=0),
    )
    return step


def per_device(psi, left_ops, right_ops, term_count, right_slot, sector, sign_bit):
    sectors, rows, m = psi.shape
    rights = right_ops.shape[0]
    f32, bf16 = jnp.float32, jnp.bfloat16
    shape = jax.ShapeDtypeStruct
    left = shifted(left_ops[0], "yh", 2)
    right_z = shifted(right_ops, "zl", 1)
    psi_z = from_next_pair(psi)
    psi_c = shifted(psi, "c", 1)
    right_c = shifted(right_ops, "c", 1)

    is_live = lax.iota(jnp.int32, right_slot.shape[0]) < term_count[0]
    weight = jnp.where(is_live, 2.0 * sign_bit.astype(f32) - 1.0, 0.0)
    in_sector = sector[None, :] == lax.iota(jnp.int32, sectors)[:, None]
    in_slot = right_slot[None, :] == lax.iota(jnp.int32, rights)[:, None]
    hit = in_sector[:, None, :] & in_slot[None, :, :]
    mixing = shifted(jnp.sum(jnp.where(hit, weight, 0.0), axis=-1), "yh", 2)

    psi_zc = shifted(psi_z, "c", 1)
    right_zc = shifted(right_z, "c", 1)

    place = jnp.stack([lax.axis_index("zl"), lax.axis_index("c")]).astype(jnp.int32)
    product_flops = 2 * sectors * rows * m * m
    prepared = shape((sectors, 2 * rows, m), bf16)
    psi_h, psi_l = call(split_kernel, (prepared, prepared), [SMEM] + [VMEM] * 2, MIB)(
        place, psi, psi_c
    )
    near = call(near_kernel, shape((sectors, rows, m), f32), [SMEM] + [VMEM] * 3, 3 * product_flops // 2)(
        place, left, psi_h, psi_l
    )
    inner = shape((sectors, rows, m), bf16)
    next_h, next_l = call(next_kernel, (inner, inner), [VMEM], MIB)(psi_z)
    inner_h, inner_l = call(
        far_kernel,
        (inner, inner),
        [SMEM] + [VMEM] * 5,
        3 * product_flops // 2,
    )(place, left, near, next_h, next_l, psi_zc)
    tall = call(
        term_kernel,
        shape((8, 4, 24, sectors * rows), f32),
        [SMEM, SMEM, VMEM, VMEM] + [pl.BlockSpec(memory_space=pl.ANY)] * 3 + [VMEM],
        3 * product_flops,
        [
            pltpu.VMEM((4, rows, sectors * rows), f32),
            pltpu.VMEM((3, rights, rows, m), f32),
            pltpu.SemaphoreType.DMA((3,)),
        ],
    )(place, mixing, inner_h, inner_l, right_ops, right_c, right_z, right_zc)

    got = lax.all_to_all(tall.reshape(8, -1, sectors * rows), ("x", "yl"), 0, 0, tiled=True)
    small = got.sum(axis=0).reshape(16, -1, sectors * rows)
    own = lax.all_to_all(small, ("yh", "zh"), 0, 0, tiled=True).sum(axis=0)
    return own.reshape(-1, sectors, rows).transpose(1, 2, 0)


def solution(mesh):
    finer = Mesh(mesh.devices.reshape(SIZES), FINE)
    placed = (
        P(None, ROWS, None),
        P(TERMS, ROWS, None),
        P(TERMS, ROWS, None),
        P(TERMS),
        P(TERMS),
        P(TERMS),
        P(TERMS),
    )
    return jax.shard_map(
        per_device, mesh=finer, in_specs=placed, out_specs=P(None, ROWS, TERMS), check_vma=False
    )
```

```python
import jax
import jax.numpy as jnp
from jax import lax
from jax.experimental import pallas as pl
from jax.experimental.pallas import tpu as pltpu
from jax.sharding import Mesh
from jax.sharding import PartitionSpec as P


FINE = ("yh", "yl", "zh", "x", "zl", "c")
SIZES = (4, 2, 4, 4, 2, 2)
TERMS = FINE[:4]
ROWS = FINE[4:]
VMEM = pl.BlockSpec(memory_space=pltpu.VMEM)
SMEM = pl.BlockSpec(memory_space=pltpu.SMEM)
MIB = 1 << 20
GROUPS = ((3, 0), (1, 2))


def shifted(block, axis, distance):
    n = lax.axis_size(axis)
    return lax.ppermute(block, axis, [(i, (i + distance) % n) for i in range(n)])


def from_next_pair(block):
    n = lax.axis_size(("zh", "zl"))
    return lax.ppermute(
        block, ("zh", "zl"), [(z, (z + (1 if z % 2 else -1)) % n) for z in range(n)]
    )


def halves(value):
    high = value.astype(jnp.bfloat16)
    return high, (value - high.astype(jnp.float32)).astype(jnp.bfloat16)


def product(a, b, dims):
    return lax.dot_general(a, b, (dims, ((), ())), preferred_element_type=jnp.float32)


def three_pass(a, b, dims):
    return product(a[0], b[0], dims) + (product(a[0], b[1], dims) + product(a[1], b[0], dims))


def mixed(mix, block, s):
    return mix[s, 0] * block[0] + mix[s, 1] * block[1]


ROW = ((1,), (0,))
TURNED = ((1,), (1,))


def split_kernel(place, psi, psi_c, psi_h, psi_l):
    sectors, rows, _ = psi.shape
    for i, p in enumerate((psi, psi_c)):
        at = pl.ds(pl.multiple_of((place[1] ^ i) * rows, rows), rows)
        for s in range(sectors):
            psi_h[s, at, :], psi_l[s, at, :] = halves(p[s])


def next_kernel(psi_z, next_h, next_l):
    for s in range(psi_z.shape[0]):
        next_h[s], next_l[s] = halves(psi_z[s])


def inner_kernel(place, left, psi_h, psi_l, next_h, next_l, psi_zc, inner_h, inner_l):
    sectors, rows, _ = psi_zc.shape
    half = 2 * rows
    mine = left[:, pl.ds(pl.multiple_of(place[0] * half, 128), half)]
    other = left[:, pl.ds(pl.multiple_of((1 - place[0]) * half, 128), half)]
    swapped = jnp.concatenate([other[:, rows:], other[:, :rows]], axis=1)
    other = jnp.where(place[1] == 1, swapped, other)
    columns = halves(jnp.concatenate([mine, other], axis=1))
    for s in range(sectors):
        zc_h, zc_l = halves(psi_zc[s])
        all_h = jnp.concatenate([psi_h[s], next_h[s], zc_h], axis=0)
        all_l = jnp.concatenate([psi_l[s], next_l[s], zc_l], axis=0)
        inner_h[s], inner_l[s] = halves(three_pass(columns, (all_h, all_l), ROW))


def term_kernel(place, mix, inner_h, inner_l, right, right_c, right_z, right_zc, out, part, held, sems):
    sectors, rows, _ = inner_h.shape
    mine = place[0] * 2 + place[1]
    fetches = [
        pltpu.make_async_copy(block, held.at[i], sems.at[i])
        for i, block in enumerate((right, right_c, right_z))
    ]
    for fetch in fetches:
        fetch.start()
    for group in GROUPS:
        blocks = []
        for i in group:
            if i < 3:
                fetches[i].wait()
            blocks.append(right_zc if i == 3 else held.at[i])
        both = []
        for s in range(sectors):
            parts = [halves(mixed(mix, block, s)) for block in blocks]
            comb = [jnp.concatenate(p, axis=0) for p in zip(*parts)]
            both.append(three_pass(comb, (inner_h[s], inner_l[s]), TURNED))
        for n, i in enumerate(group):
            rows_at = slice(n * rows, (n + 1) * rows)
            part[i] = jnp.concatenate([b[rows_at] for b in both], axis=1)
            for yl in range(2):
                for zh in range(4):
                    for x in range(4):
                        at = yl * 96 + zh * 24 + x * 6
                        out[yl * 4 + x, mine ^ i, zh * 6 : zh * 6 + 6, :] = part[i, at : at + 6, :]


def call(kernel, shapes, specs, flops, scratch=()):
    step = pl.pallas_call(
        kernel,
        out_shape=shapes,
        in_specs=specs,
        out_specs=jax.tree.map(lambda _: VMEM, shapes),
        scratch_shapes=scratch,
        compiler_params=pltpu.CompilerParams(vmem_limit_bytes=24 * MIB),
        cost_estimate=pl.CostEstimate(flops=flops, bytes_accessed=8 * MIB, transcendentals=0),
    )
    return step


def per_device(psi, left_ops, right_ops, term_count, right_slot, sector, sign_bit):
    sectors, rows, m = psi.shape
    rights = right_ops.shape[0]
    f32, bf16 = jnp.float32, jnp.bfloat16
    shape = jax.ShapeDtypeStruct
    left = shifted(left_ops[0], "yh", 2)
    right_z = shifted(right_ops, "zl", 1)
    psi_z = from_next_pair(psi)
    psi_c = shifted(psi, "c", 1)
    right_c = shifted(right_ops, "c", 1)

    is_live = lax.iota(jnp.int32, right_slot.shape[0]) < term_count[0]
    weight = jnp.where(is_live, 2.0 * sign_bit.astype(f32) - 1.0, 0.0)
    in_sector = sector[None, :] == lax.iota(jnp.int32, sectors)[:, None]
    in_slot = right_slot[None, :] == lax.iota(jnp.int32, rights)[:, None]
    hit = in_sector[:, None, :] & in_slot[None, :, :]
    mixing = shifted(jnp.sum(jnp.where(hit, weight, 0.0), axis=-1), "yh", 2)

    psi_zc = shifted(psi_z, "c", 1)
    right_zc = shifted(right_z, "c", 1)

    place = jnp.stack([lax.axis_index("zl"), lax.axis_index("c")]).astype(jnp.int32)
    product_flops = 2 * sectors * rows * m * m
    prepared = shape((sectors, 2 * rows, m), bf16)
    psi_h, psi_l = call(split_kernel, (prepared, prepared), [SMEM] + [VMEM] * 2, MIB)(
        place, psi, psi_c
    )
    inner = shape((sectors, rows, m), bf16)
    next_h, next_l = call(next_kernel, (inner, inner), [VMEM], MIB)(psi_z)
    inner_h, inner_l = call(
        inner_kernel, (inner, inner), [SMEM] + [VMEM] * 6, 3 * product_flops
    )(place, left, psi_h, psi_l, next_h, next_l, psi_zc)
    tall = call(
        term_kernel,
        shape((8, 4, 24, sectors * rows), f32),
        [SMEM, SMEM, VMEM, VMEM] + [pl.BlockSpec(memory_space=pl.ANY)] * 3 + [VMEM],
        3 * product_flops,
        [
            pltpu.VMEM((4, rows, sectors * rows), f32),
            pltpu.VMEM((3, rights, rows, m), f32),
            pltpu.SemaphoreType.DMA((3,)),
        ],
    )(place, mixing, inner_h, inner_l, right_ops, right_c, right_z, right_zc)

    got = lax.all_to_all(tall.reshape(8, -1, sectors * rows), ("yl", "x"), 0, 0, tiled=True)
    small = got.sum(axis=0).reshape(16, -1, sectors * rows)
    own = lax.all_to_all(small, ("yh", "zh"), 0, 0, tiled=True).sum(axis=0)
    return own.reshape(-1, sectors, rows).transpose(1, 2, 0)


def solution(mesh):
    finer = Mesh(mesh.devices.reshape(SIZES), FINE)
    placed = (
        P(None, ROWS, None),
        P(TERMS, ROWS, None),
        P(TERMS, ROWS, None),
        P(TERMS),
        P(TERMS),
        P(TERMS),
        P(TERMS),
    )
    return jax.shard_map(
        per_device, mesh=finer, in_specs=placed, out_specs=P(None, ROWS, TERMS), check_vma=False
    )
```
